32 devices in a mesh: row: 4 (over x, core), col: 8 (over z, y).
Axes of the slice: x: 2, y: 2, z: 4, core: 2. Of those that a mesh axis runs over, the one named last changes fastest.
Arguments:
- features: bfloat16 [4096, 256], P(('row', 'col')), may hold values from -192 to 192
- grad_out: bfloat16 [4096, 256], P(('row', 'col')), may hold values from -192 to 192
- tile_weight: bfloat16 [2048, 128, 128], P(('row', 'col')), may hold values from 0 to 256, as said below
- tile_list: int32 [128, 3, 32], P(('row', 'col')), may hold values from -1 to 63, as said below
Outputs:
- aggregated: bfloat16 [4096, 256], P(('row', 'col'))
- feature_grad: bfloat16 [4096, 256], P(('row', 'col'))
The draws below stay inside these ranges and needn't reach their ends.
Inputs may be any that keep to these rules, and one draw needn't show every extreme that they name: `tile_list`: each column of a list is a slot (tile number, source block below 1, destination block below 8); tile number -1 marks an empty slot, whose blocks are 0. The tile numbers listed by one device are distinct and are 0 to n - 1 for some n between 40 and 64; some device lists all 64. On every device some step has all 32 slots used. Stored tiles that no slot lists take no part. `tile_weight`: entries are whole numbers.
All inputs are finite; a program needn't handle non-finite values.
Results may differ from the reference program's by a relative error of at most 0.017.
Values may be sent and summed in bfloat16 or wider, within the bound.
No kernel may reach another device: no remote copies, remote signals or barrier semaphores. Data moves between devices by JAX's collectives and lax.ppermute only.
A program may use at most 64 MiB of HBM per device.

```python
import jax
import jax.numpy as jnp
from jax import lax

HID = 256
TILE = 128
SB = 1
DB = 1
TILES_DEV = 64
MAXT = 32
ND = 4096
NS = 4096
N_ROW = 4
N_COL = 8


def layout_tables(key):
    base = jax.random.fold_in(key, 11)
    devices = N_ROW * N_COL
    slot_count = N_ROW * MAXT
    lowest = TILES_DEV * 5 // 8
    full_dev = jax.random.randint(jax.random.fold_in(base, 1), (), 0, devices)

    def one_device(dev_index):
        keys = jax.random.split(jax.random.fold_in(base, 100 + dev_index), 6)
        hot_step = jax.random.randint(keys[0], (), 0, N_ROW)
        tile_total = jax.random.randint(keys[1], (), lowest, TILES_DEV + 1)
        tile_total = jnp.where(dev_index == full_dev, TILES_DEV, tile_total)
        slot_order = jax.random.permutation(keys[2], slot_count).astype(jnp.int32)
        step_of = jnp.arange(slot_count, dtype=jnp.int32) // MAXT
        priority = jnp.where(step_of == hot_step, slot_order - slot_count, slot_order)
        slot_rank = jnp.argsort(jnp.argsort(priority, stable=True), stable=True).astype(jnp.int32)
        chosen = slot_rank < tile_total
        second = jax.random.permutation(keys[3], slot_count).astype(jnp.int32)
        second = jnp.where(chosen, second, second + slot_count)
        tile_ident = jnp.argsort(jnp.argsort(second, stable=True), stable=True).astype(jnp.int32)
        tile_number = jnp.where(chosen, tile_ident, -1)
        source = jnp.where(chosen, jax.random.randint(keys[4], (slot_count,), 0, SB), 0)
        target = jnp.where(chosen, jax.random.randint(keys[5], (slot_count,), 0, N_COL * DB), 0)
        slot_table = jnp.stack([tile_number, source, target]).astype(jnp.int32).reshape(3, N_ROW, MAXT)
        return jnp.transpose(slot_table, (1, 0, 2))
    return jax.vmap(one_device)(jnp.arange(devices, dtype=jnp.int32))


def draw_tile_list(key, part):
    return layout_tables(key).reshape(N_ROW * N_COL * N_ROW, 3, MAXT)


def draw_tile_weight(key, part):
    tables = layout_tables(key)
    devices = N_ROW * N_COL
    level_key = jax.random.fold_in(key, 23)
    dst_level = jnp.left_shift(1, jax.random.randint(jax.random.fold_in(level_key, 1), (ND,), 0, 5)).astype(jnp.int32)
    src_level = jnp.left_shift(1, jax.random.randint(jax.random.fold_in(level_key, 2), (NS,), 0, 5)).astype(jnp.int32)
    node_offset = jnp.arange(TILE, dtype=jnp.int32)
    step_of = jnp.arange(N_ROW * MAXT, dtype=jnp.int32) // MAXT
    tile_range = jnp.arange(TILES_DEV, dtype=jnp.int32)

    def one_device(dev_index):
        slot_table = tables[dev_index]
        row_pos = dev_index // N_COL
        col_pos = dev_index % N_COL
        tile_ids = slot_table[:, 0, :].reshape(-1)
        matches = (tile_ids[None, :] == tile_range[:, None]).astype(jnp.int32)
        tile_step = jnp.sum(matches * step_of[None, :], axis=1)
        tile_src = jnp.sum(matches * slot_table[:, 1, :].reshape(-1)[None, :], axis=1)
        tile_dst = jnp.sum(matches * slot_table[:, 2, :].reshape(-1)[None, :], axis=1)
        owner_row = (row_pos - tile_step) % N_ROW
        src_rows = ((owner_row * N_COL + col_pos) * SB + tile_src)[:, None] * TILE + node_offset
        dst_rows = (row_pos * N_COL * DB + tile_dst)[:, None] * TILE + node_offset
        row_level = dst_level[dst_rows]
        col_level = src_level[src_rows]
        random_bits = jax.random.randint(jax.random.fold_in(key, 1000 + dev_index), (TILES_DEV, TILE, TILE), 0, 1 << 20)
        first_count = random_bits % 1024 % (row_level[:, :, None] + 1)
        second_count = random_bits // 1024 % (col_level[:, None, :] + 1)
        return (first_count * second_count).astype(jnp.float32).astype(jnp.bfloat16)
    drawn = lax.map(one_device, jnp.arange(devices, dtype=jnp.int32))
    return drawn.reshape(devices * TILES_DEV, TILE, TILE)


def block_levels(stream_key, shape, pieces, least, high):
    def one(axis_at, shards_of):
        steps = jax.random.uniform(jax.random.fold_in(jax.random.fold_in(stream_key, 6), axis_at), (shards_of,), jnp.float32, least / len(pieces), high / len(pieces))
        return jnp.repeat(jnp.exp(steps), shape[axis_at] // shards_of).reshape((-1,) + (1,) * (len(shape) - axis_at - 1))

    gain = one(*pieces[0])
    for cut in pieces[1:]:
        gain = gain * one(*cut)
    return gain


def normal_values(key, shape, scale, most, cuts=(), kind=jnp.bfloat16):
    result = scale * jax.random.normal(key, shape, jnp.float32)
    if cuts:
        result = result * block_levels(key, shape, cuts, -0.22, 0.18)
    return jnp.clip(result, -most, most).astype(kind)


def setup_inputs(seed: int = 0) -> dict:
    splits = jax.random.split(jax.random.key(seed), 5)
    return {
        "features": normal_values(splits[0], (NS, HID), 32.0, 192.0, ((0, 32),)),
        "grad_out": normal_values(splits[1], (ND, HID), 32.0, 192.0, ((0, 32),)),
        "tile_weight": draw_tile_weight(jax.random.fold_in(splits[4], 71), 0),
        "tile_list": draw_tile_list(jax.random.fold_in(splits[4], 71), 0),
    }


def reference(features, grad_out, tile_weight, tile_list):
    devices = N_ROW * N_COL
    lists = tile_list.reshape(devices, N_ROW, 3, MAXT)
    tiles = tile_weight.reshape(devices, TILES_DEV, TILE, TILE)
    node_offset = jnp.arange(TILE, dtype=jnp.int32)
    step_pos = jnp.arange(N_ROW, dtype=jnp.int32)[:, None]
    group_rows = N_COL * DB * TILE

    def geometry(dev_index):
        row_pos = dev_index // N_COL
        col_pos = dev_index % N_COL
        tile_ids = lists[dev_index, :, 0, :]
        keep_mask = (tile_ids >= 0).astype(jnp.bfloat16)
        owner_row = (row_pos - step_pos) % N_ROW
        src_block = (owner_row * N_COL + col_pos) * SB + lists[dev_index, :, 1, :]
        dst_local = lists[dev_index, :, 2, :]
        weights = tiles[dev_index][jnp.maximum(tile_ids, 0)] * keep_mask[:, :, None, None]
        src_rows = src_block[:, :, None] * TILE + node_offset
        dst_rows = dst_local[:, :, None] * TILE + node_offset
        return (row_pos, weights, src_rows, dst_rows)

    def degree_pass(carry, dev_index):
        dst_sum, src_sum = carry
        row_pos, weights, src_rows, dst_rows = geometry(dev_index)
        weights_f = weights.astype(jnp.float32)
        dst_sum = dst_sum.at[row_pos * group_rows + dst_rows].add(lax.optimization_barrier(jnp.sum(weights_f, axis=3)))
        src_sum = src_sum.at[src_rows].add(lax.optimization_barrier(jnp.sum(weights_f, axis=2)))
        return ((dst_sum, src_sum), None)
    indices = jnp.arange(devices, dtype=jnp.int32)
    start_sums = (jnp.zeros((ND,), jnp.float32), jnp.zeros((NS,), jnp.float32))
    (dst_sum, src_sum), unused = lax.scan(degree_pass, start_sums, indices)
    dst_scale = lax.rsqrt(1.0 + dst_sum)
    src_scale = lax.rsqrt(1.0 + src_sum)
    scaled = (features.astype(jnp.float32) * src_scale[:, None]).astype(jnp.bfloat16)
    scaled_grads = (grad_out.astype(jnp.float32) * dst_scale[:, None]).astype(jnp.bfloat16)

    def forward_pass(totals, dev_index):
        row_pos, weights, src_rows, dst_rows = geometry(dev_index)
        products = jnp.einsum('skij,skjf->skif', weights.astype(jnp.float32), scaled[src_rows].astype(jnp.float32))
        partial_value = jnp.zeros((group_rows, HID), jnp.float32).at[dst_rows].add(products)
        partial_value = lax.optimization_barrier(partial_value.astype(jnp.bfloat16)).astype(jnp.float32)
        first_row = row_pos * group_rows
        current = lax.dynamic_slice_in_dim(totals, first_row, group_rows, 0)
        totals = lax.dynamic_update_slice_in_dim(totals, current + partial_value, first_row, 0)
        return (totals, None)

    def backward_pass(grads, dev_index):
        row_pos, weights, src_rows, dst_rows = geometry(dev_index)
        picked = scaled_grads[row_pos * group_rows + dst_rows]
        products = jnp.einsum('skij,skif->skjf', weights.astype(jnp.float32), picked.astype(jnp.float32))
        return (grads.at[src_rows].add(products), None)
    totals, unused = lax.scan(forward_pass, jnp.zeros((ND, HID), jnp.float32), indices)
    grads, unused = lax.scan(backward_pass, jnp.zeros((NS, HID), jnp.float32), indices)
    aggregated = (totals * dst_scale[:, None]).astype(jnp.bfloat16)
    feature_grad = (grads * src_scale[:, None]).astype(jnp.bfloat16)
    return (aggregated, feature_grad)
```

```python
import functools

import jax
import jax.numpy as jnp
from jax import lax
from jax.experimental import pallas as pl
from jax.experimental.pallas import tpu as pltpu
from jax.sharding import PartitionSpec as P

F32 = jnp.float32
BF16 = jnp.bfloat16
PARTS = 3


def round_up(value, step):
    return -(-value // step) * step


def message_rows(count, width):
    part_rows = count // width
    return part_rows, round_up(PARTS * part_rows, 16)


def pack_counts(counts, width):
    rows, total = counts.shape
    part_rows = total // width
    row = lax.broadcasted_iota(jnp.int32, (rows, width), 0)
    value = jnp.zeros((rows, width), F32)
    for i in range(part_rows):
        here = row == i
        for part in range(1, PARTS):
            here = here | (row == part * part_rows + i)
        value = jnp.where(here, counts[:, i * width : (i + 1) * width], value)
    high = value.astype(BF16).astype(F32)
    middle = (value - high).astype(BF16).astype(F32)
    low = value - high - middle
    packed = jnp.where(row < part_rows, high, jnp.where(row < 2 * part_rows, middle, low))
    return packed.astype(BF16)


def unpack_scales(parts, part_rows):
    total = parts[0:part_rows]
    for part in range(1, PARTS):
        total = total + parts[part * part_rows : (part + 1) * part_rows]
    return lax.rsqrt(1.0 + total)


def scale_column(scales, block, tile_len):
    width = scales.shape[1]
    row, first = divmod(block * tile_len, width)
    line = scales[row : row + 1, first : first + tile_len]
    return jnp.broadcast_to(line, (tile_len, tile_len)).T


def scaled_rows(rows, column):
    width = rows.shape[1]
    tile_len = column.shape[1]
    pieces = [
        rows[:, i * tile_len : (i + 1) * tile_len].astype(F32) * column
        for i in range(width // tile_len)
    ]
    return jnp.concatenate(pieces, axis=1)


def place_kernel(
    chunks,
    src_blocks,
    list_ref,
    features_ref,
    grads_ref,
    tiles_hbm,
    adjacency_ref,
    src_send_ref,
    dst_send_ref,
    tiles_ref,
    total_ref,
    line_ref,
    where_ref,
    sems,
):
    tile_count, tile_len, _ = tiles_ref.shape
    step_count, _, slot_count = list_ref.shape
    width = features_ref.shape[1]
    dst_blocks = adjacency_ref.shape[0] // tile_len
    slots = adjacency_ref.shape[1] // tile_len
    pairs = dst_blocks * slots
    per_chunk = tile_count // chunks

    def chunk_copy(i):
        window = pl.ds(i * per_chunk, per_chunk)
        return pltpu.make_async_copy(tiles_hbm.at[window], tiles_ref.at[window], sems.at[i])

    for i in range(chunks):
        chunk_copy(i).start()

    @pl.loop(0, tile_count)
    def _(t):
        where_ref[t] = pairs

    row_pos = lax.axis_index("row")
    for step in range(step_count):
        owner = lax.rem(row_pos - step + step_count, step_count)

        @pl.loop(0, slot_count)
        def _(k):
            t = list_ref[step, 0, k]
            pair = list_ref[step, 2, k] * slots + owner * src_blocks + list_ref[step, 1, k]
            where_ref[jnp.where(t >= 0, t, tile_count)] = pair

    @pl.loop(0, pairs)
    def _(p):
        total_ref[p] = jnp.zeros((tile_len, tile_len), F32)

    total_ref[pairs] = jnp.zeros((tile_len, tile_len), F32)
    for i in range(chunks):
        chunk_copy(i).wait()

        @pl.loop(i * per_chunk, (i + 1) * per_chunk)
        def _(t):
            p = where_ref[t]
            total_ref[p] = total_ref[p] + tiles_ref[t].astype(F32)

    src_rows = src_send_ref.shape[1] - features_ref.shape[0]
    dst_rows = dst_send_ref.shape[1] - grads_ref.shape[0]
    col_sums = tuple(jnp.zeros((8, tile_len), F32) for _ in range(slots))

    def block_row(e, sums):
        first = pl.multiple_of(e * tile_len, tile_len)
        across = jnp.zeros((tile_len, tile_len), F32)
        out = []
        for s in range(slots):
            block = total_ref[e * slots + s]
            adjacency_ref[pl.ds(first, tile_len), s * tile_len : (s + 1) * tile_len] = block.astype(
                BF16
            )
            across = across + block
            out.append(sums[s] + jnp.sum(block.reshape(tile_len // 8, 8, tile_len), axis=0))
        high = across.astype(BF16)
        low = (across - high.astype(F32)).astype(BF16)
        ones = jnp.ones((dst_rows, tile_len), BF16)
        contract = (((1,), (1,)), ((), ()))
        line_ref[:, pl.ds(first, tile_len)] = lax.dot_general(
            ones, high, contract, preferred_element_type=F32
        ) + lax.dot_general(ones, low, contract, preferred_element_type=F32)
        return tuple(out)

    if dst_blocks <= 8:
        for e in range(dst_blocks):
            col_sums = block_row(e, col_sums)
    else:
        col_sums = lax.fori_loop(0, dst_blocks, block_row, col_sums)
    src_line = jnp.concatenate(
        [
            jnp.broadcast_to(jnp.sum(sums, axis=0, keepdims=True), (src_rows, tile_len))
            for sums in col_sums
        ],
        axis=1,
    )
    src_packed = pack_counts(src_line, width)
    dst_packed = pack_counts(line_ref[...], width)
    for j in range(src_send_ref.shape[0]):
        src_send_ref[j, : features_ref.shape[0]] = features_ref[...]
        src_send_ref[j, features_ref.shape[0] :] = src_packed
    for j in range(dst_send_ref.shape[0]):
        dst_send_ref[j, : grads_ref.shape[0]] = grads_ref[...]
        dst_send_ref[j, grads_ref.shape[0] :] = dst_packed


def forward_kernel(
    src_blocks, message_ref, adjacency_ref, partial_ref, own_scale_ref, scaled_ref
):
    senders, rows, width = message_ref.shape
    dst_blocks, tile_len, _ = partial_ref.shape
    body = src_blocks * tile_len
    part_rows = senders * body // width
    parts = message_ref[0, body:].astype(F32)
    for j in range(1, senders):
        parts = parts + message_ref[j, body:].astype(F32)
    scales = unpack_scales(parts, part_rows)
    row_pos = lax.axis_index("row")
    for j in range(senders):
        for b in range(src_blocks):
            column = scale_column(scales, j * src_blocks + b, tile_len)
            first = (j * src_blocks + b) * tile_len
            rows_here = message_ref[j, b * tile_len : (b + 1) * tile_len]
            scaled_ref[first : first + tile_len] = scaled_rows(rows_here, column).astype(BF16)

            @pl.when(row_pos == j)
            def _():
                own_scale_ref[b * tile_len : (b + 1) * tile_len] = column

    def one(e):
        first = pl.multiple_of(e * tile_len, tile_len)
        partial_ref[e] = jnp.dot(
            adjacency_ref[pl.ds(first, tile_len)], scaled_ref[...], preferred_element_type=F32
        ).astype(BF16)

    if dst_blocks <= 8:
        for e in range(dst_blocks):
            one(e)
    else:
        pl.loop(0, dst_blocks)(one)


def backward_kernel(
    own_blocks, message_ref, adjacency_ref, partial_ref, own_scale_ref, scaled_ref
):
    senders, rows, width = message_ref.shape
    slots, tile_len, _ = partial_ref.shape
    body = own_blocks * tile_len
    part_rows = senders * body // width
    parts = message_ref[0, body:].astype(F32)
    for j in range(1, senders):
        parts = parts + message_ref[j, body:].astype(F32)
    scales = unpack_scales(parts, part_rows)
    col_pos = lax.axis_index("col")
    for j in range(senders):
        for b in range(own_blocks):
            column = scale_column(scales, j * own_blocks + b, tile_len)
            first = (j * own_blocks + b) * tile_len
            rows_here = message_ref[j, b * tile_len : (b + 1) * tile_len]
            scaled_ref[first : first + tile_len] = scaled_rows(rows_here, column).astype(BF16)

            @pl.when(col_pos == j)
            def _():
                own_scale_ref[b * tile_len : (b + 1) * tile_len] = column

    for s in range(slots):
        partial_ref[s] = lax.dot_general(
            adjacency_ref[:, s * tile_len : (s + 1) * tile_len],
            scaled_ref[...],
            (((0,), (0,)), ((), ())),
            preferred_element_type=F32,
        ).astype(BF16)


def finish_kernel(received_ref, scale_ref, out_ref):
    senders, rows, width = received_ref.shape
    tile_len = scale_ref.shape[1]
    total = received_ref[0].astype(F32)
    for j in range(1, senders):
        total = total + received_ref[j].astype(F32)
    column = scale_ref[...]
    for i in range(width // tile_len):
        lanes = slice(i * tile_len, (i + 1) * tile_len)
        out_ref[:, lanes] = (total[:, lanes] * column).astype(BF16)


VMEM = pl.BlockSpec(memory_space=pltpu.VMEM)


def local(features, grad_out, tile_weight, tile_list):
    row_count = lax.axis_size("row")
    col_count = lax.axis_size("col")
    tile_count, tile_len, _ = tile_weight.shape
    width = features.shape[1]
    src_blocks = features.shape[0] // tile_len
    own_blocks = grad_out.shape[0] // tile_len
    slots = row_count * src_blocks
    dst_blocks = col_count * own_blocks
    _, src_rows = message_rows(slots * tile_len, width)
    _, dst_rows = message_rows(dst_blocks * tile_len, width)
    chunks = 4 if tile_count % 4 == 0 else 1
    shape = jax.ShapeDtypeStruct

    adjacency, src_send, dst_send = pl.pallas_call(
        functools.partial(place_kernel, chunks, src_blocks),
        out_shape=(
            shape((dst_blocks * tile_len, slots * tile_len), BF16),
            shape((row_count, features.shape[0] + src_rows, width), BF16),
            shape((col_count, grad_out.shape[0] + dst_rows, width), BF16),
        ),
        in_specs=[
            pl.BlockSpec(memory_space=pltpu.SMEM),
            VMEM,
            VMEM,
            pl.BlockSpec(memory_space=pl.ANY),
        ],
        out_specs=(VMEM, VMEM, VMEM),
        scratch_shapes=[
            pltpu.VMEM((tile_count, tile_len, tile_len), BF16),
            pltpu.VMEM((dst_blocks * slots + 1, tile_len, tile_len), F32),
            pltpu.VMEM((dst_rows, dst_blocks * tile_len), F32),
            pltpu.SMEM((tile_count + 1,), jnp.int32),
            pltpu.SemaphoreType.DMA((chunks,)),
        ],
        name="place",
    )(tile_list, features, grad_out, tile_weight)

    src_message = lax.all_to_all(src_send, "row", 0, 0, tiled=True)
    dst_message = lax.all_to_all(dst_send, "col", 0, 0, tiled=True)
    partial, src_scale = pl.pallas_call(
        functools.partial(forward_kernel, src_blocks),
        out_shape=(
            shape((dst_blocks, tile_len, width), BF16),
            shape((features.shape[0], tile_len), F32),
        ),
        in_specs=[VMEM, VMEM],
        out_specs=(VMEM, VMEM),
        scratch_shapes=[pltpu.VMEM((slots * tile_len, width), BF16)],
        name="forward",
    )(src_message, adjacency)
    dst_partials = lax.all_to_all(partial, "col", 0, 0, tiled=True)
    back_partial, dst_scale = pl.pallas_call(
        functools.partial(backward_kernel, own_blocks),
        out_shape=(
            shape((slots, tile_len, width), BF16),
            shape((grad_out.shape[0], tile_len), F32),
        ),
        in_specs=[VMEM, VMEM],
        out_specs=(VMEM, VMEM),
        scratch_shapes=[pltpu.VMEM((dst_blocks * tile_len, width), BF16)],
        name="backward",
    )(dst_message, adjacency)
    src_partials = lax.all_to_all(back_partial, "row", 0, 0, tiled=True)

    def finish(received, scale, count, rows):
        return pl.pallas_call(
            finish_kernel,
            out_shape=shape((rows, width), BF16),
            in_specs=[VMEM, VMEM],
            out_specs=VMEM,
            name="finish",
        )(received.reshape(count, rows, width), scale)

    feature_grad = finish(src_partials, src_scale, row_count, features.shape[0])
    aggregated = finish(dst_partials, dst_scale, col_count, grad_out.shape[0])
    return (aggregated, feature_grad)


def solution(mesh):
    return jax.shard_map(
        local,
        mesh=mesh,
        in_specs=(
            P(("row", "col"), None),
            P(("row", "col"), None),
            P(("row", "col"), None, None),
            P(("row", "col"), None, None),
        ),
        out_specs=(P(("row", "col"), None), P(("row", "col"), None)),
        check_vma=False,
    )
```

```python
import functools

import jax
import jax.numpy as jnp
from jax import lax
from jax.experimental import pallas as pl
from jax.experimental.pallas import tpu as pltpu
from jax.sharding import PartitionSpec as P


F32 = jnp.float32
BF16 = jnp.bfloat16
PARTS = 3


def round_up(value, step):
    return -(-value // step) * step


def meet(here, k, count):
    if count & (count - 1) == 0:
        return here ^ k, here ^ k
    return lax.rem(here + k, count), lax.rem(here - k + count, count)


def exchange(value, axis, k):
    count = lax.axis_size(axis)
    if count & (count - 1) == 0:
        pairs = [(source, source ^ k) for source in range(count)]
    else:
        pairs = [(source, (source + k) % count) for source in range(count)]
    return lax.ppermute(value, axis, pairs)


def message_rows(count, width):
    part_rows = count // width
    return part_rows, round_up(PARTS * part_rows, 16)


def pack_counts(counts, width):
    rows, total = counts.shape
    part_rows = total // width
    row = lax.broadcasted_iota(jnp.int32, (rows, width), 0)
    value = jnp.zeros((rows, width), F32)
    for i in range(part_rows):
        here = row == i
        for part in range(1, PARTS):
            here = here | (row == part * part_rows + i)
        value = jnp.where(here, counts[:, i * width : (i + 1) * width], value)
    high = value.astype(BF16).astype(F32)
    middle = (value - high).astype(BF16).astype(F32)
    low = value - high - middle
    packed = jnp.where(row < part_rows, high, jnp.where(row < 2 * part_rows, middle, low))
    return packed.astype(BF16)


def scale_rows(messages, places, tile_len, scales_ref, scaled_ref, own_scale_ref):
    senders = len(messages)
    width = messages[0].shape[1]
    body = own_scale_ref.shape[0]
    part_rows = senders * body // width
    parts = messages[0][body:].astype(F32)
    for message_ref in messages[1:]:
        parts = parts + message_ref[body:].astype(F32)
    total = parts[0:part_rows]
    for part in range(1, PARTS):
        total = total + parts[part * part_rows : (part + 1) * part_rows]
    scales = lax.rsqrt(1.0 + total)
    for block in range(senders * body // tile_len):
        row, first = divmod(block * tile_len, width)
        scales_ref[block : block + 1] = scales[row : row + 1, first : first + tile_len]
    for index, (message_ref, place) in enumerate(zip(messages, places)):
        for b in range(body // tile_len):
            block = place * (body // tile_len) + b
            line = scales_ref[pl.ds(block, 1)]
            column = jnp.broadcast_to(line, (tile_len, tile_len)).T
            rows_here = message_ref[b * tile_len : (b + 1) * tile_len]
            first = pl.multiple_of(block * tile_len, tile_len)
            scaled_ref[pl.ds(first, tile_len)] = scaled_rows(rows_here, column).astype(BF16)
            if index == 0:
                own_scale_ref[b * tile_len : (b + 1) * tile_len] = column


def scaled_rows(rows, column):
    width = rows.shape[1]
    tile_len = column.shape[1]
    pieces = [
        rows[:, i * tile_len : (i + 1) * tile_len].astype(F32) * column
        for i in range(width // tile_len)
    ]
    return jnp.concatenate(pieces, axis=1)


def place_kernel(
    chunks,
    src_blocks,
    list_hbm,
    features_hbm,
    grads_hbm,
    tiles_hbm,
    adjacency_ref,
    src_send_ref,
    dst_send_ref,
    tiles_ref,
    total_ref,
    line_ref,
    list_ref,
    where_ref,
    sems,
):
    tile_count, tile_len, _ = tiles_ref.shape
    _, step_count, slot_count = list_ref.shape
    width = features_hbm.shape[1]
    dst_blocks = adjacency_ref.shape[0] // tile_len
    slots = adjacency_ref.shape[1] // tile_len
    pairs = dst_blocks * slots
    per_chunk = tile_count // chunks

    def chunk_copy(i):
        window = pl.ds(i * per_chunk, per_chunk)
        return pltpu.make_async_copy(tiles_hbm.at[window], tiles_ref.at[window], sems.at[i])

    list_copy = pltpu.make_async_copy(list_hbm, list_ref, sems.at[chunks])
    row_copies = [
        pltpu.make_async_copy(
            features_hbm, src_send_ref.at[pl.ds(0, features_hbm.shape[0])], sems.at[chunks + 1]
        ),
        pltpu.make_async_copy(
            grads_hbm, dst_send_ref.at[pl.ds(0, grads_hbm.shape[0])], sems.at[chunks + 2]
        ),
    ]
    list_copy.start()
    for i in range(chunks):
        chunk_copy(i).start()
    for copy in row_copies:
        copy.start()

    @pl.loop(0, pairs + 1)
    def _(p):
        total_ref[p] = jnp.zeros((tile_len, tile_len), F32)

    @pl.loop(0, tile_count, unroll=8 if tile_count % 8 == 0 else 1)
    def _(t):
        where_ref[t] = pairs

    list_copy.wait()
    row_pos = lax.axis_index("row")
    for step in range(step_count):
        first = lax.rem(row_pos - step + step_count, step_count) * src_blocks

        @pl.loop(0, slot_count, unroll=8 if slot_count % 8 == 0 else 1)
        def _(k):
            t = list_ref[0, step, k]
            pair = list_ref[2, step, k] * slots + first + list_ref[1, step, k]
            where_ref[jnp.where(t >= 0, t, tile_count)] = pair

    for i in range(chunks):
        chunk_copy(i).wait()

        @pl.loop(i * per_chunk, (i + 1) * per_chunk, unroll=4 if per_chunk % 4 == 0 else 1)
        def _(t):
            p = where_ref[t]
            total_ref[p] = total_ref[p] + tiles_ref[t].astype(F32)

    src_rows = src_send_ref.shape[0] - features_hbm.shape[0]
    dst_rows = dst_send_ref.shape[0] - grads_hbm.shape[0]
    col_sums = tuple(jnp.zeros((8, tile_len), F32) for _ in range(slots))

    def block_row(e, sums):
        first = pl.multiple_of(e * tile_len, tile_len)
        across = jnp.zeros((tile_len, tile_len), F32)
        out = []
        for s in range(slots):
            block = total_ref[e * slots + s]
            adjacency_ref[pl.ds(first, tile_len), s * tile_len : (s + 1) * tile_len] = block.astype(
                BF16
            )
            across = across + block
            out.append(sums[s] + jnp.sum(block.reshape(tile_len // 8, 8, tile_len), axis=0))
        high = across.astype(BF16)
        low = (across - high.astype(F32)).astype(BF16)
        ones = jnp.ones((dst_rows, tile_len), BF16)
        contract = (((1,), (1,)), ((), ()))
        line_ref[:, pl.ds(first, tile_len)] = lax.dot_general(
            ones, high, contract, preferred_element_type=F32
        ) + lax.dot_general(ones, low, contract, preferred_element_type=F32)
        return tuple(out)

    if dst_blocks <= 8:
        for e in range(dst_blocks):
            col_sums = block_row(e, col_sums)
    else:
        col_sums = lax.fori_loop(0, dst_blocks, block_row, col_sums)
    src_line = jnp.concatenate(
        [
            jnp.broadcast_to(jnp.sum(sums, axis=0, keepdims=True), (src_rows, tile_len))
            for sums in col_sums
        ],
        axis=1,
    )
    src_packed = pack_counts(src_line, width)
    dst_packed = pack_counts(line_ref[...], width)
    src_send_ref[features_hbm.shape[0] :] = src_packed
    dst_send_ref[grads_hbm.shape[0] :] = dst_packed
    for copy in row_copies:
        copy.wait()


def forward_kernel(senders, receivers, own_rows, *refs):
    messages, adjacency_ref = refs[:senders], refs[senders]
    partial_refs = refs[senders + 1 : senders + 1 + receivers]
    own_scale_ref, scales_ref, scaled_ref = refs[senders + 1 + receivers :]
    rows = partial_refs[0].shape[0]
    row_pos = lax.axis_index("row")
    places = [meet(row_pos, k, senders)[1] for k in range(senders)]
    scale_rows(messages, places, own_scale_ref.shape[1], scales_ref, scaled_ref, own_scale_ref)
    col_pos = lax.axis_index("col")
    for k, partial_ref in enumerate(partial_refs):
        near = meet(col_pos, k, receivers)[0]
        for half in range(rows // own_rows):
            block = near ^ receivers if half else near
            first = pl.multiple_of(block * own_rows, own_rows)
            partial_ref[half * own_rows : (half + 1) * own_rows] = jnp.dot(
                adjacency_ref[pl.ds(first, own_rows)], scaled_ref[...], preferred_element_type=F32
            ).astype(partial_ref.dtype)


def backward_kernel(senders, receivers, halves, *refs):
    messages, adjacency_ref = refs[:senders], refs[senders]
    partial_refs = refs[senders + 1 : senders + 1 + receivers]
    own_scale_ref, scales_ref, scaled_ref = refs[senders + 1 + receivers :]
    src_rows = partial_refs[0].shape[0]
    group = senders // halves
    col_pos = lax.axis_index("col")
    places = [meet(col_pos, k, group)[1] for k in range(group)]
    if halves == 2:
        places = places + [place ^ group for place in places]
    scale_rows(messages, places, own_scale_ref.shape[1], scales_ref, scaled_ref, own_scale_ref)
    row_pos = lax.axis_index("row")
    for k, partial_ref in enumerate(partial_refs):
        first = pl.multiple_of(meet(row_pos, k, receivers)[0] * src_rows, src_rows)
        partial_ref[...] = lax.dot_general(
            adjacency_ref[:, pl.ds(first, src_rows)],
            scaled_ref[...],
            (((0,), (0,)), ((), ())),
            preferred_element_type=F32,
        ).astype(partial_ref.dtype)


def merge_kernel(*refs):
    *pieces, near_ref, far_ref = refs
    rows = near_ref.shape[0]
    for half, out_ref in enumerate((near_ref, far_ref)):
        window = slice(half * rows, (half + 1) * rows)
        total = pieces[0][window].astype(F32)
        for piece in pieces[1:]:
            total = total + piece[window].astype(F32)
        out_ref[...] = total.astype(out_ref.dtype)


def finish_kernel(*refs):
    *pieces, scale_ref, out_ref = refs
    width = out_ref.shape[1]
    tile_len = scale_ref.shape[1]
    terms = []
    for piece in pieces:
        terms += [piece[...]] if len(piece.shape) == 2 else [piece[j] for j in range(piece.shape[0])]
    total = terms[0].astype(F32)
    for term in terms[1:]:
        total = total + term.astype(F32)
    column = scale_ref[...]
    for i in range(width // tile_len):
        lanes = slice(i * tile_len, (i + 1) * tile_len)
        out_ref[:, lanes] = (total[:, lanes] * column).astype(BF16)


def room(size):
    return pltpu.CompilerParams(vmem_limit_bytes=min(size + (4 << 20), 60 * 1024 * 1024))


VMEM = pl.BlockSpec(memory_space=pltpu.VMEM)


def aggregate(features, grad_out, tile_weight, tile_list):
    row_count = lax.axis_size("row")
    col_count = lax.axis_size("col")
    tile_count, tile_len, _ = tile_weight.shape
    width = features.shape[1]
    src_blocks = features.shape[0] // tile_len
    own_blocks = grad_out.shape[0] // tile_len
    slots = row_count * src_blocks
    dst_blocks = col_count * own_blocks
    _, src_rows = message_rows(slots * tile_len, width)
    _, dst_rows = message_rows(dst_blocks * tile_len, width)
    chunks = 4 if tile_count % 4 == 0 else 1
    shape = jax.ShapeDtypeStruct
    block = tile_len * tile_len
    dense = dst_blocks * slots * block
    rows_in = (slots + 2 * dst_blocks) * tile_len * width
    FORWARD = 3 * dense + 8 * rows_in
    BACKWARD = 3 * dense + 8 * rows_in
    FINISH = 4 * rows_in

    adjacency, src_send, dst_send = pl.pallas_call(
        functools.partial(place_kernel, chunks, src_blocks),
        out_shape=(
            shape((dst_blocks * tile_len, slots * tile_len), BF16),
            shape((features.shape[0] + src_rows, width), BF16),
            shape((grad_out.shape[0] + dst_rows, width), BF16),
        ),
        in_specs=[pl.BlockSpec(memory_space=pltpu.HBM)] * 4,
        out_specs=(VMEM, VMEM, VMEM),
        scratch_shapes=[
            pltpu.VMEM((tile_count, tile_len, tile_len), BF16),
            pltpu.VMEM((dst_blocks * slots + 1, tile_len, tile_len), F32),
            pltpu.VMEM((dst_rows, dst_blocks * tile_len), F32),
            pltpu.SMEM((tile_list.shape[1], row_count, tile_list.shape[2]), jnp.int32),
            pltpu.SMEM((tile_count + 1,), jnp.int32),
            pltpu.SemaphoreType.DMA((chunks + 3,)),
        ],
        compiler_params=room(60 * 1024 * 1024),
        name="place",
    )(jnp.transpose(tile_list, (1, 0, 2)), features, grad_out, tile_weight)

    own_rows = grad_out.shape[0]
    halves = 2 if col_count >= 4 and col_count & (col_count - 1) == 0 else 1
    group = col_count // halves

    def near(value, k):
        if halves == 1:
            return exchange(value, "col", k)
        return lax.ppermute(value, "col", [(c, c ^ k) for c in range(col_count)])

    src_messages = [src_send] + [exchange(src_send, "row", k) for k in range(1, row_count)]
    if halves == 2:
        far_send = exchange(dst_send, "col", group)
    dst_messages = [dst_send] + [near(dst_send, k) for k in range(1, group)]
    if halves == 2:
        dst_messages += [far_send] + [near(far_send, k) for k in range(1, group)]

    *partials, src_scale = pl.pallas_call(
        functools.partial(forward_kernel, row_count, group, own_rows),
        out_shape=(
            *(shape((halves * own_rows, width), BF16 if k else F32) for k in range(group)),
            shape((features.shape[0], tile_len), F32),
        ),
        in_specs=[VMEM] * (row_count + 1),
        out_specs=(VMEM,) * (group + 1),
        scratch_shapes=[
            pltpu.VMEM((slots, tile_len), F32),
            pltpu.VMEM((slots * tile_len, width), BF16),
        ],
        compiler_params=room(FORWARD),
        name="forward",
    )(*src_messages, adjacency)
    dst_partials = partials[:1] + [near(partials[k], k) for k in range(1, group)]
    if halves == 2:
        kept, sent = pl.pallas_call(
            merge_kernel,
            out_shape=(shape((own_rows, width), F32), shape((own_rows, width), BF16)),
            in_specs=[VMEM] * group,
            out_specs=(VMEM, VMEM),
            compiler_params=room(FINISH),
            name="merge",
        )(*dst_partials)
        dst_partials = [kept, exchange(sent, "col", group)]
    *back_partials, dst_scale = pl.pallas_call(
        functools.partial(backward_kernel, col_count, row_count, halves),
        out_shape=(
            *(
                shape((features.shape[0], width), BF16 if k else F32)
                for k in range(row_count)
            ),
            shape((grad_out.shape[0], tile_len), F32),
        ),
        in_specs=[VMEM] * (col_count + 1),
        out_specs=(VMEM,) * (row_count + 1),
        scratch_shapes=[
            pltpu.VMEM((dst_blocks, tile_len), F32),
            pltpu.VMEM((dst_blocks * tile_len, width), BF16),
        ],
        compiler_params=room(BACKWARD),
        name="backward",
    )(*dst_messages, adjacency)
    src_partials = back_partials[:1] + [
        exchange(back_partials[k], "row", k) for k in range(1, row_count)
    ]

    def finish(received, scale, rows):
        return pl.pallas_call(
            finish_kernel,
            out_shape=shape((rows, width), BF16),
            in_specs=[VMEM] * (len(received) + 1),
            out_specs=VMEM,
            compiler_params=room(FINISH),
            name="finish",
        )(*received, scale)

    feature_grad = finish(src_partials, src_scale, features.shape[0])
    aggregated = finish(dst_partials, dst_scale, grad_out.shape[0])
    return (aggregated, feature_grad)


def solution(mesh):
    return jax.shard_map(
        aggregate,
        mesh=mesh,
        in_specs=(
            P(("row", "col"), None),
            P(("row", "col"), None),
            P(("row", "col"), None, None),
            P(("row", "col"), None, None),
        ),
        out_specs=(P(("row", "col"), None), P(("row", "col"), None)),
        check_vma=False,
    )
```

```python
import functools

import jax
import jax.numpy as jnp
from jax import lax
from jax.experimental import pallas as pl
from jax.experimental.pallas import tpu as pltpu
from jax.sharding import PartitionSpec as P


F32 = jnp.float32
BF16 = jnp.bfloat16
PARTS = 3


def round_up(value, step):
    return -(-value // step) * step


def meet(here, k, count):
    if count & (count - 1) == 0:
        return here ^ k, here ^ k
    return lax.rem(here + k, count), lax.rem(here - k + count, count)


def exchange(value, axis, k):
    count = lax.axis_size(axis)
    if count & (count - 1) == 0:
        pairs = [(source, source ^ k) for source in range(count)]
    else:
        pairs = [(source, (source + k) % count) for source in range(count)]
    return lax.ppermute(value, axis, pairs)


def message_rows(count, width):
    part_rows = count // width
    return part_rows, round_up(PARTS * part_rows, 16)


def pack_counts(counts, width):
    rows, total = counts.shape
    part_rows = total // width
    row = lax.broadcasted_iota(jnp.int32, (rows, width), 0)
    value = jnp.zeros((rows, width), F32)
    for i in range(part_rows):
        here = row == i
        for part in range(1, PARTS):
            here = here | (row == part * part_rows + i)
        value = jnp.where(here, counts[:, i * width : (i + 1) * width], value)
    high = value.astype(BF16).astype(F32)
    middle = (value - high).astype(BF16).astype(F32)
    low = value - high - middle
    packed = jnp.where(row < part_rows, high, jnp.where(row < 2 * part_rows, middle, low))
    return packed.astype(BF16)


def scale_rows(messages, places, tile_len, scales_ref, scaled_ref, own_scale_ref):
    senders = len(messages)
    width = messages[0].shape[1]
    body = own_scale_ref.shape[0]
    part_rows = senders * body // width
    parts = messages[0][body:].astype(F32)
    for message_ref in messages[1:]:
        parts = parts + message_ref[body:].astype(F32)
    total = parts[0:part_rows]
    for part in range(1, PARTS):
        total = total + parts[part * part_rows : (part + 1) * part_rows]
    scales = lax.rsqrt(1.0 + total)
    for block in range(senders * body // tile_len):
        row, first = divmod(block * tile_len, width)
        scales_ref[block : block + 1] = scales[row : row + 1, first : first + tile_len]
    for index, (message_ref, place) in enumerate(zip(messages, places)):
        for b in range(body // tile_len):
            block = place * (body // tile_len) + b
            line = scales_ref[pl.ds(block, 1)]
            column = jnp.broadcast_to(line, (tile_len, tile_len)).T
            rows_here = message_ref[b * tile_len : (b + 1) * tile_len]
            first = pl.multiple_of(block * tile_len, tile_len)
            scaled_ref[pl.ds(first, tile_len)] = scaled_rows(rows_here, column).astype(BF16)
            if index == 0:
                own_scale_ref[b * tile_len : (b + 1) * tile_len] = column


def scaled_rows(rows, column):
    width = rows.shape[1]
    tile_len = column.shape[1]
    pieces = [
        rows[:, i * tile_len : (i + 1) * tile_len].astype(F32) * column
        for i in range(width // tile_len)
    ]
    return jnp.concatenate(pieces, axis=1)


def place_kernel(
    chunks,
    src_blocks,
    list_hbm,
    features_hbm,
    grads_hbm,
    tiles_hbm,
    adjacency_ref,
    src_send_ref,
    dst_send_ref,
    tiles_ref,
    total_ref,
    line_ref,
    list_ref,
    where_ref,
    sems,
):
    tile_count, tile_len, _ = tiles_ref.shape
    _, step_count, slot_count = list_ref.shape
    width = features_hbm.shape[1]
    dst_blocks = adjacency_ref.shape[0] // tile_len
    slots = adjacency_ref.shape[1] // tile_len
    pairs = dst_blocks * slots
    per_chunk = tile_count // chunks

    def chunk_copy(i):
        window = pl.ds(i * per_chunk, per_chunk)
        return pltpu.make_async_copy(tiles_hbm.at[window], tiles_ref.at[window], sems.at[i])

    list_copy = pltpu.make_async_copy(list_hbm, list_ref, sems.at[chunks])
    row_copies = [
        pltpu.make_async_copy(
            features_hbm, src_send_ref.at[pl.ds(0, features_hbm.shape[0])], sems.at[chunks + 1]
        ),
        pltpu.make_async_copy(
            grads_hbm, dst_send_ref.at[pl.ds(0, grads_hbm.shape[0])], sems.at[chunks + 2]
        ),
    ]
    list_copy.start()
    for i in range(chunks):
        chunk_copy(i).start()
    for copy in row_copies:
        copy.start()

    @pl.loop(0, pairs + 1)
    def _(p):
        total_ref[p] = jnp.zeros((tile_len, tile_len), F32)

    @pl.loop(0, tile_count, unroll=8 if tile_count % 8 == 0 else 1)
    def _(t):
        where_ref[t] = pairs

    list_copy.wait()
    row_pos = lax.axis_index("row")
    for step in range(step_count):
        first = lax.rem(row_pos - step + step_count, step_count) * src_blocks

        @pl.loop(0, slot_count, unroll=8 if slot_count % 8 == 0 else 1)
        def _(k):
            t = list_ref[0, step, k]
            pair = list_ref[2, step, k] * slots + first + list_ref[1, step, k]
            where_ref[jnp.where(t >= 0, t, tile_count)] = pair

    for i in range(chunks):
        chunk_copy(i).wait()

        @pl.loop(i * per_chunk, (i + 1) * per_chunk, unroll=4 if per_chunk % 4 == 0 else 1)
        def _(t):
            p = where_ref[t]
            total_ref[p] = total_ref[p] + tiles_ref[t].astype(F32)

    src_rows = src_send_ref.shape[0] - features_hbm.shape[0]
    dst_rows = dst_send_ref.shape[0] - grads_hbm.shape[0]
    col_sums = tuple(jnp.zeros((8, tile_len), F32) for _ in range(slots))

    def block_row(e, sums):
        first = pl.multiple_of(e * tile_len, tile_len)
        across = jnp.zeros((tile_len, tile_len), F32)
        out = []
        for s in range(slots):
            block = total_ref[e * slots + s]
            adjacency_ref[pl.ds(first, tile_len), s * tile_len : (s + 1) * tile_len] = block.astype(
                BF16
            )
            across = across + block
            out.append(sums[s] + jnp.sum(block.reshape(tile_len // 8, 8, tile_len), axis=0))
        high = across.astype(BF16)
        low = (across - high.astype(F32)).astype(BF16)
        ones = jnp.ones((dst_rows, tile_len), BF16)
        contract = (((1,), (1,)), ((), ()))
        line_ref[:, pl.ds(first, tile_len)] = lax.dot_general(
            ones, high, contract, preferred_element_type=F32
        ) + lax.dot_general(ones, low, contract, preferred_element_type=F32)
        return tuple(out)

    if dst_blocks <= 8:
        for e in range(dst_blocks):
            col_sums = block_row(e, col_sums)
    else:
        col_sums = lax.fori_loop(0, dst_blocks, block_row, col_sums)
    src_line = jnp.concatenate(
        [
            jnp.broadcast_to(jnp.sum(sums, axis=0, keepdims=True), (src_rows, tile_len))
            for sums in col_sums
        ],
        axis=1,
    )
    src_packed = pack_counts(src_line, width)
    dst_packed = pack_counts(line_ref[...], width)
    src_send_ref[features_hbm.shape[0] :] = src_packed
    dst_send_ref[grads_hbm.shape[0] :] = dst_packed
    for copy in row_copies:
        copy.wait()


def forward_kernel(senders, receivers, own_rows, *refs):
    messages, adjacency_ref = refs[:senders], refs[senders]
    partial_refs = refs[senders + 1 : senders + 1 + receivers]
    own_scale_ref, scales_ref, scaled_ref = refs[senders + 1 + receivers :]
    rows = partial_refs[0].shape[0]
    row_pos = lax.axis_index("row")
    places = [meet(row_pos, k, senders)[1] for k in range(senders)]
    scale_rows(messages, places, own_scale_ref.shape[1], scales_ref, scaled_ref, own_scale_ref)
    col_pos = lax.axis_index("col")
    for k, partial_ref in enumerate(partial_refs):
        near = meet(col_pos, k, receivers)[0]
        for half in range(rows // own_rows):
            block = near ^ receivers if half else near
            first = pl.multiple_of(block * own_rows, own_rows)
            partial_ref[half * own_rows : (half + 1) * own_rows] = jnp.dot(
                adjacency_ref[pl.ds(first, own_rows)], scaled_ref[...], preferred_element_type=F32
            ).astype(partial_ref.dtype)


def backward_kernel(senders, receivers, halves, *refs):
    messages, adjacency_ref = refs[:senders], refs[senders]
    partial_refs = refs[senders + 1 : senders + 1 + receivers]
    own_scale_ref, scales_ref, scaled_ref = refs[senders + 1 + receivers :]
    src_rows = partial_refs[0].shape[0]
    group = senders // halves
    col_pos = lax.axis_index("col")
    places = [meet(col_pos, k, group)[1] for k in range(group)]
    if halves == 2:
        places = places + [place ^ group for place in places]
    scale_rows(messages, places, own_scale_ref.shape[1], scales_ref, scaled_ref, own_scale_ref)
    row_pos = lax.axis_index("row")
    for k, partial_ref in enumerate(partial_refs):
        first = pl.multiple_of(meet(row_pos, k, receivers)[0] * src_rows, src_rows)
        partial_ref[...] = lax.dot_general(
            adjacency_ref[:, pl.ds(first, src_rows)],
            scaled_ref[...],
            (((0,), (0,)), ((), ())),
            preferred_element_type=F32,
        ).astype(partial_ref.dtype)


def merge_kernel(*refs):
    *pieces, near_ref, far_ref = refs
    rows = near_ref.shape[0]
    for half, out_ref in enumerate((near_ref, far_ref)):
        window = slice(half * rows, (half + 1) * rows)
        total = pieces[0][window].astype(F32)
        for piece in pieces[1:]:
            total = total + piece[window].astype(F32)
        out_ref[...] = total.astype(out_ref.dtype)


def finish_kernel(*refs):
    *pieces, scale_ref, out_ref = refs
    width = out_ref.shape[1]
    tile_len = scale_ref.shape[1]
    terms = []
    for piece in pieces:
        terms += [piece[...]] if len(piece.shape) == 2 else [piece[j] for j in range(piece.shape[0])]
    total = terms[0].astype(F32)
    for term in terms[1:]:
        total = total + term.astype(F32)
    column = scale_ref[...]
    for i in range(width // tile_len):
        lanes = slice(i * tile_len, (i + 1) * tile_len)
        out_ref[:, lanes] = (total[:, lanes] * column).astype(BF16)


def room(size):
    return pltpu.CompilerParams(vmem_limit_bytes=min(size + (4 << 20), 60 * 1024 * 1024))


VMEM = pl.BlockSpec(memory_space=pltpu.VMEM)


def aggregate(features, grad_out, tile_weight, tile_list):
    row_count = lax.axis_size("row")
    col_count = lax.axis_size("col")
    tile_count, tile_len, _ = tile_weight.shape
    width = features.shape[1]
    src_blocks = features.shape[0] // tile_len
    own_blocks = grad_out.shape[0] // tile_len
    slots = row_count * src_blocks
    dst_blocks = col_count * own_blocks
    _, src_rows = message_rows(slots * tile_len, width)
    _, dst_rows = message_rows(dst_blocks * tile_len, width)
    chunks = 4 if tile_count % 4 == 0 else 1
    shape = jax.ShapeDtypeStruct
    block = tile_len * tile_len
    dense = dst_blocks * slots * block
    rows_in = (slots + 2 * dst_blocks) * tile_len * width
    PLACE = 2 * tile_count * block + 6 * dense + 8 * rows_in
    FORWARD = 3 * dense + 8 * rows_in
    BACKWARD = 3 * dense + 8 * rows_in
    FINISH = 4 * rows_in

    adjacency, src_send, dst_send = pl.pallas_call(
        functools.partial(place_kernel, chunks, src_blocks),
        out_shape=(
            shape((dst_blocks * tile_len, slots * tile_len), BF16),
            shape((features.shape[0] + src_rows, width), BF16),
            shape((grad_out.shape[0] + dst_rows, width), BF16),
        ),
        in_specs=[pl.BlockSpec(memory_space=pltpu.HBM)] * 4,
        out_specs=(VMEM, VMEM, VMEM),
        scratch_shapes=[
            pltpu.VMEM((tile_count, tile_len, tile_len), BF16),
            pltpu.VMEM((dst_blocks * slots + 1, tile_len, tile_len), F32),
            pltpu.VMEM((dst_rows, dst_blocks * tile_len), F32),
            pltpu.SMEM((tile_list.shape[1], row_count, tile_list.shape[2]), jnp.int32),
            pltpu.SMEM((tile_count + 1,), jnp.int32),
            pltpu.SemaphoreType.DMA((chunks + 3,)),
        ],
        compiler_params=room(PLACE),
        name="place",
    )(
        *(
            pltpu.with_memory_space_constraint(operand, pltpu.HBM)
            for operand in (jnp.transpose(tile_list, (1, 0, 2)), features, grad_out, tile_weight)
        )
    )

    own_rows = grad_out.shape[0]
    halves = 2 if col_count >= 4 and col_count & (col_count - 1) == 0 else 1
    group = col_count // halves

    def near(value, k):
        if halves == 1:
            return exchange(value, "col", k)
        return lax.ppermute(value, "col", [(c, c ^ k) for c in range(col_count)])

    src_messages = [src_send] + [exchange(src_send, "row", k) for k in range(1, row_count)]
    if halves == 2:
        far_send = exchange(dst_send, "col", group)
    dst_messages = [dst_send] + [near(dst_send, k) for k in range(1, group)]
    if halves == 2:
        dst_messages += [far_send] + [near(far_send, k) for k in range(1, group)]

    *partials, src_scale = pl.pallas_call(
        functools.partial(forward_kernel, row_count, group, own_rows),
        out_shape=(
            *(shape((halves * own_rows, width), BF16 if k else F32) for k in range(group)),
            shape((features.shape[0], tile_len), F32),
        ),
        in_specs=[VMEM] * (row_count + 1),
        out_specs=(VMEM,) * (group + 1),
        scratch_shapes=[
            pltpu.VMEM((slots, tile_len), F32),
            pltpu.VMEM((slots * tile_len, width), BF16),
        ],
        compiler_params=room(FORWARD),
        name="forward",
    )(*src_messages, adjacency)
    dst_partials = partials[:1] + [near(partials[k], k) for k in range(1, group)]
    if halves == 2:
        kept, sent = pl.pallas_call(
            merge_kernel,
            out_shape=(shape((own_rows, width), F32), shape((own_rows, width), BF16)),
            in_specs=[VMEM] * group,
            out_specs=(VMEM, VMEM),
            compiler_params=room(FINISH),
            name="merge",
        )(*dst_partials)
        dst_partials = [kept, exchange(sent, "col", group)]
    *back_partials, dst_scale = pl.pallas_call(
        functools.partial(backward_kernel, col_count, row_count, halves),
        out_shape=(
            *(
                shape((features.shape[0], width), BF16 if k else F32)
                for k in range(row_count)
            ),
            shape((grad_out.shape[0], tile_len), F32),
        ),
        in_specs=[VMEM] * (col_count + 1),
        out_specs=(VMEM,) * (row_count + 1),
        scratch_shapes=[
            pltpu.VMEM((dst_blocks, tile_len), F32),
            pltpu.VMEM((dst_blocks * tile_len, width), BF16),
        ],
        compiler_params=room(BACKWARD),
        name="backward",
    )(*dst_messages, adjacency)
    src_partials = back_partials[:1] + [
        exchange(back_partials[k], "row", k) for k in range(1, row_count)
    ]

    def finish(received, scale, rows):
        return pl.pallas_call(
            finish_kernel,
            out_shape=shape((rows, width), BF16),
            in_specs=[VMEM] * (len(received) + 1),
            out_specs=VMEM,
            compiler_params=room(FINISH),
            name="finish",
        )(*received, scale)

    feature_grad = finish(src_partials, src_scale, features.shape[0])
    aggregated = finish(dst_partials, dst_scale, grad_out.shape[0])
    return (aggregated, feature_grad)


def solution(mesh):
    return jax.shard_map(
        aggregate,
        mesh=mesh,
        in_specs=(
            P(("row", "col"), None),
            P(("row", "col"), None),
            P(("row", "col"), None, None),
            P(("row", "col"), None, None),
        ),
        out_specs=(P(("row", "col"), None), P(("row", "col"), None)),
        check_vma=False,
    )
```

```python
import functools

import jax
import jax.numpy as jnp
from jax import lax
from jax.experimental import pallas as pl
from jax.experimental.pallas import tpu as pltpu
from jax.sharding import PartitionSpec as P


F32 = jnp.float32
BF16 = jnp.bfloat16
PARTS = 3


def round_up(value, step):
    return -(-value // step) * step


def meet(here, k, count):
    if count & (count - 1) == 0:
        return here ^ k, here ^ k
    return lax.rem(here + k, count), lax.rem(here - k + count, count)


def exchange(value, axis, k):
    count = lax.axis_size(axis)
    if count & (count - 1) == 0:
        pairs = [(source, source ^ k) for source in range(count)]
    else:
        pairs = [(source, (source + k) % count) for source in range(count)]
    return lax.ppermute(value, axis, pairs)


def message_rows(count, width):
    part_rows = count // width
    return part_rows, round_up(PARTS * part_rows, 16)


def pack_counts(counts, width):
    rows, total = counts.shape
    part_rows = total // width
    row = lax.broadcasted_iota(jnp.int32, (rows, width), 0)
    value = jnp.zeros((rows, width), F32)
    for i in range(part_rows):
        here = row == i
        for part in range(1, PARTS):
            here = here | (row == part * part_rows + i)
        value = jnp.where(here, counts[:, i * width : (i + 1) * width], value)
    high = value.astype(BF16).astype(F32)
    middle = (value - high).astype(BF16).astype(F32)
    low = value - high - middle
    packed = jnp.where(row < part_rows, high, jnp.where(row < 2 * part_rows, middle, low))
    return packed.astype(BF16)


def scale_rows(messages, places, tile_len, scales_ref, scaled_ref, own_scale_ref):
    senders = len(messages)
    width = messages[0].shape[1]
    body = own_scale_ref.shape[0]
    part_rows = senders * body // width
    parts = messages[0][body:].astype(F32)
    for message_ref in messages[1:]:
        parts = parts + message_ref[body:].astype(F32)
    total = parts[0:part_rows]
    for part in range(1, PARTS):
        total = total + parts[part * part_rows : (part + 1) * part_rows]
    scales = lax.rsqrt(1.0 + total)
    for block in range(senders * body // tile_len):
        row, first = divmod(block * tile_len, width)
        scales_ref[block : block + 1] = scales[row : row + 1, first : first + tile_len]
    for index, (message_ref, place) in enumerate(zip(messages, places)):
        for b in range(body // tile_len):
            block = place * (body // tile_len) + b
            line = scales_ref[pl.ds(block, 1)]
            column = jnp.broadcast_to(line, (tile_len, tile_len)).T
            rows_here = message_ref[b * tile_len : (b + 1) * tile_len]
            first = pl.multiple_of(block * tile_len, tile_len)
            scaled_ref[pl.ds(first, tile_len)] = scaled_rows(rows_here, column).astype(BF16)
            if index == 0:
                own_scale_ref[b * tile_len : (b + 1) * tile_len] = column


def scaled_rows(rows, column):
    width = rows.shape[1]
    tile_len = column.shape[1]
    pieces = [
        rows[:, i * tile_len : (i + 1) * tile_len].astype(F32) * column
        for i in range(width // tile_len)
    ]
    return jnp.concatenate(pieces, axis=1)


def place_kernel(
    chunks,
    src_blocks,
    list_hbm,
    features_hbm,
    grads_hbm,
    tiles_hbm,
    adjacency_ref,
    src_send_ref,
    dst_send_ref,
    tiles_ref,
    total_ref,
    line_ref,
    list_ref,
    where_ref,
    sems,
):
    tile_count, tile_len, _ = tiles_ref.shape
    _, step_count, slot_count = list_ref.shape
    width = features_hbm.shape[1]
    dst_blocks = adjacency_ref.shape[0] // tile_len
    slots = adjacency_ref.shape[1] // tile_len
    pairs = dst_blocks * slots
    per_chunk = tile_count // chunks

    def chunk_copy(i):
        window = pl.ds(i * per_chunk, per_chunk)
        return pltpu.make_async_copy(tiles_hbm.at[window], tiles_ref.at[window], sems.at[i])

    list_copy = pltpu.make_async_copy(list_hbm, list_ref, sems.at[chunks])
    row_copies = [
        pltpu.make_async_copy(
            features_hbm, src_send_ref.at[pl.ds(0, features_hbm.shape[0])], sems.at[chunks + 1]
        ),
        pltpu.make_async_copy(
            grads_hbm, dst_send_ref.at[pl.ds(0, grads_hbm.shape[0])], sems.at[chunks + 2]
        ),
    ]
    list_copy.start()
    for i in range(chunks):
        chunk_copy(i).start()
    for copy in row_copies:
        copy.start()

    @pl.loop(0, pairs + 1, unroll=3 if (pairs + 1) % 3 == 0 else 1)
    def _(p):
        total_ref[p] = jnp.zeros((tile_len, tile_len), F32)

    @pl.loop(0, tile_count, unroll=32 if tile_count % 32 == 0 else 1)
    def _(t):
        where_ref[t] = pairs

    list_copy.wait()
    row_pos = lax.axis_index("row")
    for step in range(step_count):
        first = lax.rem(row_pos - step + step_count, step_count) * src_blocks

        @pl.loop(0, slot_count, unroll=32 if slot_count % 32 == 0 else 1)
        def _(k):
            t = list_ref[0, step, k]
            pair = list_ref[2, step, k] * slots + first + list_ref[1, step, k]
            where_ref[jnp.where(t >= 0, t, tile_count)] = pair

    for i in range(chunks):
        chunk_copy(i).wait()

        @pl.loop(i * per_chunk, (i + 1) * per_chunk, unroll=8 if per_chunk % 8 == 0 else 1)
        def _(t):
            p = where_ref[t]
            total_ref[p] = total_ref[p] + tiles_ref[t].astype(F32)

    src_rows = src_send_ref.shape[0] - features_hbm.shape[0]
    dst_rows = dst_send_ref.shape[0] - grads_hbm.shape[0]
    col_sums = tuple(jnp.zeros((8, tile_len), F32) for _ in range(slots))

    def block_row(e, sums):
        first = pl.multiple_of(e * tile_len, tile_len)
        across = jnp.zeros((tile_len, tile_len), F32)
        out = []
        for s in range(slots):
            block = total_ref[e * slots + s]
            adjacency_ref[pl.ds(first, tile_len), s * tile_len : (s + 1) * tile_len] = block.astype(
                BF16
            )
            across = across + block
            out.append(sums[s] + jnp.sum(block.reshape(tile_len // 8, 8, tile_len), axis=0))
        high = across.astype(BF16)
        low = (across - high.astype(F32)).astype(BF16)
        ones = jnp.ones((dst_rows, tile_len), BF16)
        contract = (((1,), (1,)), ((), ()))
        line_ref[:, pl.ds(first, tile_len)] = lax.dot_general(
            ones, high, contract, preferred_element_type=F32
        ) + lax.dot_general(ones, low, contract, preferred_element_type=F32)
        return tuple(out)

    if dst_blocks <= 8:
        for e in range(dst_blocks):
            col_sums = block_row(e, col_sums)
    else:
        col_sums = lax.fori_loop(0, dst_blocks, block_row, col_sums)
    src_line = jnp.concatenate(
        [
            jnp.broadcast_to(jnp.sum(sums, axis=0, keepdims=True), (src_rows, tile_len))
            for sums in col_sums
        ],
        axis=1,
    )
    src_packed = pack_counts(src_line, width)
    dst_packed = pack_counts(line_ref[...], width)
    src_send_ref[features_hbm.shape[0] :] = src_packed
    dst_send_ref[grads_hbm.shape[0] :] = dst_packed
    for copy in row_copies:
        copy.wait()


def forward_kernel(senders, receivers, own_rows, *refs):
    messages, adjacency_ref = refs[:senders], refs[senders]
    partial_refs = refs[senders + 1 : senders + 1 + receivers]
    own_scale_ref, scales_ref, scaled_ref = refs[senders + 1 + receivers :]
    rows = partial_refs[0].shape[0]
    row_pos = lax.axis_index("row")
    places = [meet(row_pos, k, senders)[1] for k in range(senders)]
    scale_rows(messages, places, own_scale_ref.shape[1], scales_ref, scaled_ref, own_scale_ref)
    col_pos = lax.axis_index("col")
    for k, partial_ref in enumerate(partial_refs):
        near = meet(col_pos, k, receivers)[0]
        for half in range(rows // own_rows):
            block = near ^ receivers if half else near
            first = pl.multiple_of(block * own_rows, own_rows)
            partial_ref[half * own_rows : (half + 1) * own_rows] = jnp.dot(
                adjacency_ref[pl.ds(first, own_rows)], scaled_ref[...], preferred_element_type=F32
            ).astype(partial_ref.dtype)


def backward_kernel(senders, receivers, halves, *refs):
    messages, adjacency_ref = refs[:senders], refs[senders]
    partial_refs = refs[senders + 1 : senders + 1 + receivers]
    own_scale_ref, scales_ref, scaled_ref = refs[senders + 1 + receivers :]
    src_rows = partial_refs[0].shape[0]
    group = senders // halves
    col_pos = lax.axis_index("col")
    places = [meet(col_pos, k, group)[1] for k in range(group)]
    if halves == 2:
        places = places + [place ^ group for place in places]
    scale_rows(messages, places, own_scale_ref.shape[1], scales_ref, scaled_ref, own_scale_ref)
    row_pos = lax.axis_index("row")
    for k, partial_ref in enumerate(partial_refs):
        first = pl.multiple_of(meet(row_pos, k, receivers)[0] * src_rows, src_rows)
        partial_ref[...] = lax.dot_general(
            adjacency_ref[:, pl.ds(first, src_rows)],
            scaled_ref[...],
            (((0,), (0,)), ((), ())),
            preferred_element_type=F32,
        ).astype(partial_ref.dtype)


def merge_kernel(*refs):
    *pieces, near_ref, far_ref = refs
    rows = near_ref.shape[0]
    for half, out_ref in enumerate((near_ref, far_ref)):
        window = slice(half * rows, (half + 1) * rows)
        total = pieces[0][window].astype(F32)
        for piece in pieces[1:]:
            total = total + piece[window].astype(F32)
        out_ref[...] = total.astype(out_ref.dtype)


def finish_kernel(*refs):
    *pieces, scale_ref, out_ref = refs
    width = out_ref.shape[1]
    tile_len = scale_ref.shape[1]
    terms = []
    for piece in pieces:
        terms += [piece[...]] if len(piece.shape) == 2 else [piece[j] for j in range(piece.shape[0])]
    total = terms[0].astype(F32)
    for term in terms[1:]:
        total = total + term.astype(F32)
    column = scale_ref[...]
    for i in range(width // tile_len):
        lanes = slice(i * tile_len, (i + 1) * tile_len)
        out_ref[:, lanes] = (total[:, lanes] * column).astype(BF16)


def room(size):
    return pltpu.CompilerParams(vmem_limit_bytes=min(size + (4 << 20), 60 * 1024 * 1024))


VMEM = pl.BlockSpec(memory_space=pltpu.VMEM)


def aggregate(features, grad_out, tile_weight, tile_list):
    row_count = lax.axis_size("row")
    col_count = lax.axis_size("col")
    tile_count, tile_len, _ = tile_weight.shape
    width = features.shape[1]
    src_blocks = features.shape[0] // tile_len
    own_blocks = grad_out.shape[0] // tile_len
    slots = row_count * src_blocks
    dst_blocks = col_count * own_blocks
    _, src_rows = message_rows(slots * tile_len, width)
    _, dst_rows = message_rows(dst_blocks * tile_len, width)
    chunks = 4 if tile_count % 4 == 0 else 1
    shape = jax.ShapeDtypeStruct
    block = tile_len * tile_len
    dense = dst_blocks * slots * block
    rows_in = (slots + 2 * dst_blocks) * tile_len * width
    PLACE = 2 * tile_count * block + 6 * dense + 8 * rows_in
    FORWARD = 3 * dense + 8 * rows_in
    BACKWARD = 3 * dense + 8 * rows_in
    FINISH = 4 * rows_in

    adjacency, src_send, dst_send = pl.pallas_call(
        functools.partial(place_kernel, chunks, src_blocks),
        out_shape=(
            shape((dst_blocks * tile_len, slots * tile_len), BF16),
            shape((features.shape[0] + src_rows, width), BF16),
            shape((grad_out.shape[0] + dst_rows, width), BF16),
        ),
        in_specs=[pl.BlockSpec(memory_space=pltpu.HBM)] * 4,
        out_specs=(VMEM, VMEM, VMEM),
        scratch_shapes=[
            pltpu.VMEM((tile_count, tile_len, tile_len), BF16),
            pltpu.VMEM((dst_blocks * slots + 1, tile_len, tile_len), F32),
            pltpu.VMEM((dst_rows, dst_blocks * tile_len), F32),
            pltpu.SMEM((tile_list.shape[1], row_count, tile_list.shape[2]), jnp.int32),
            pltpu.SMEM((tile_count + 1,), jnp.int32),
            pltpu.SemaphoreType.DMA((chunks + 3,)),
        ],
        compiler_params=room(PLACE),
        name="place",
    )(
        *(
            pltpu.with_memory_space_constraint(operand, pltpu.HBM)
            for operand in (jnp.transpose(tile_list, (1, 0, 2)), features, grad_out, tile_weight)
        )
    )

    own_rows = grad_out.shape[0]
    halves = 2 if col_count >= 4 and col_count & (col_count - 1) == 0 else 1
    group = col_count // halves

    def near(value, k):
        if halves == 1:
            return exchange(value, "col", k)
        return lax.ppermute(value, "col", [(c, c ^ k) for c in range(col_count)])

    def row(value, k):
        return exchange(value, "row", k)

    src_messages = [src_send] + [row(src_send, k) for k in range(1, row_count)]
    if halves == 2:
        far_send = exchange(dst_send, "col", group)
    dst_messages = [dst_send] + [near(dst_send, k) for k in range(1, group)]
    if halves == 2:
        dst_messages += [far_send] + [near(far_send, k) for k in range(1, group)]

    *partials, src_scale = pl.pallas_call(
        functools.partial(forward_kernel, row_count, group, own_rows),
        out_shape=(
            *(shape((halves * own_rows, width), BF16 if k else F32) for k in range(group)),
            shape((features.shape[0], tile_len), F32),
        ),
        in_specs=[VMEM] * (row_count + 1),
        out_specs=(VMEM,) * (group + 1),
        scratch_shapes=[
            pltpu.VMEM((slots, tile_len), F32),
            pltpu.VMEM((slots * tile_len, width), BF16),
        ],
        compiler_params=room(FORWARD),
        name="forward",
    )(*src_messages, adjacency)
    dst_partials = partials[:1] + [near(partials[k], k) for k in range(1, group)]
    if halves == 2:
        kept, sent = pl.pallas_call(
            merge_kernel,
            out_shape=(shape((own_rows, width), F32), shape((own_rows, width), BF16)),
            in_specs=[VMEM] * group,
            out_specs=(VMEM, VMEM),
            compiler_params=room(FINISH),
            name="merge",
        )(*dst_partials)
        dst_partials = [kept, exchange(sent, "col", group)]
    *back_partials, dst_scale = pl.pallas_call(
        functools.partial(backward_kernel, col_count, row_count, halves),
        out_shape=(
            *(
                shape((features.shape[0], width), BF16 if k else F32)
                for k in range(row_count)
            ),
            shape((grad_out.shape[0], tile_len), F32),
        ),
        in_specs=[VMEM] * (col_count + 1),
        out_specs=(VMEM,) * (row_count + 1),
        scratch_shapes=[
            pltpu.VMEM((dst_blocks, tile_len), F32),
            pltpu.VMEM((dst_blocks * tile_len, width), BF16),
        ],
        compiler_params=room(BACKWARD),
        name="backward",
    )(*dst_messages, adjacency)
    src_partials = back_partials[:1] + [
        row(back_partials[k], k) for k in range(1, row_count)
    ]

    def finish(received, scale, rows):
        return pl.pallas_call(
            finish_kernel,
            out_shape=shape((rows, width), BF16),
            in_specs=[VMEM] * (len(received) + 1),
            out_specs=VMEM,
            compiler_params=room(FINISH),
            name="finish",
        )(*received, scale)

    feature_grad = finish(src_partials, src_scale, features.shape[0])
    aggregated = finish(dst_partials, dst_scale, grad_out.shape[0])
    return (aggregated, feature_grad)


def solution(mesh):
    return jax.shard_map(
        aggregate,
        mesh=mesh,
        in_specs=(
            P(("row", "col"), None),
            P(("row", "col"), None),
            P(("row", "col"), None, None),
            P(("row", "col"), None, None),
        ),
        out_specs=(P(("row", "col"), None), P(("row", "col"), None)),
        check_vma=False,
    )
```
